1024 devices in a mesh: dp: 4 (over y), section: 8 (over x, core), tensor: 32 (over z).
Axes of the slice: x: 4, y: 4, z: 32, core: 2. Of those that a mesh axis runs over, the one named last changes fastest.
Arguments:
- hidden: bfloat16 [8, 512, 8192], P('section', 'dp', 'tensor'), may hold values from -6 to 6
- q_weight: bfloat16 [8, 8192, 8192], P('section', None, 'tensor'), may hold values from -0.0625 to 0.0625
- o_weight: bfloat16 [8, 8192, 8192], P('section', 'tensor'), may hold values from -0.0625 to 0.0625
- vision_kv: bfloat16 [8, 8, 1024, 2048], P(None, None, ('dp', 'section', 'tensor')), may hold values from -6 to 6
- q_gain: float32 [8, 128], P('section'), may hold values from 1.5 to 8
- k_gain: float32 [8, 128], P('section'), may hold values from 1.5 to 8
- attn_gate: float32 [8], P('section'), may hold values from 0.25 to 1.5
- images: int32 [8], replicated, may hold values from 1 to 2
- tiles: int32 [8, 2], replicated, may hold values from 1 to 4
- text_start: int32 [8, 2], replicated, may hold values from 0 to 63
Outputs:
- layer_out: bfloat16 [8, 512, 8192], P('section', 'dp', 'tensor')
The draws below stay inside these ranges and needn't reach their ends.
All inputs are finite; a program needn't handle non-finite values.
Results may differ from the reference program's by a relative error of at most 0.02.
Values may be sent and summed in bfloat16 or wider, within the bound.
A program may use at most 64 MiB of HBM per device.

```python
import math
import jax
import jax.numpy as jnp
from jax import lax

D = 8192
H = 64
KVH = 8
HD = 128
TILES = 4
IMG = 2
P_SIZE = 128
TXT = 64
LAYERS = 8
SAMPLES = 8
VIS = 1024


def gain_draw(key):
    return jnp.exp(jax.random.uniform(key, (LAYERS, HD), jnp.float32, math.log(1.5), math.log(3.0)))


def draw_q_gain(key, part):
    return gain_draw(jax.random.fold_in(key, 11))


def draw_k_gain(key, part):
    return gain_draw(jax.random.fold_in(key, 23))


def touch_ends(drawn, key, smallest, top_value):
    extent = drawn.shape
    place = [jax.random.randint(jax.random.fold_in(key, axis), (), 0, extent[axis]) for axis in range(len(extent))]
    drawn = drawn.at[tuple(place)].set(smallest)
    longest = extent.index(max(extent))
    place[longest] = (place[longest] + 1) % extent[longest]
    return drawn.at[tuple(place)].set(top_value)


def level_of(key, extent, split, low, largest):
    loudness = 1.0
    for dim, blocks in split:
        steps = jax.random.uniform(jax.random.fold_in(jax.random.fold_in(key, 6), dim), (blocks,), jnp.float32, low / len(split), largest / len(split))
        loudness = loudness * jnp.repeat(jnp.exp(steps), extent[dim] // blocks).reshape((-1,) + (1,) * (len(extent) - 1 - dim))
    return loudness


def gaussian(rng, shape, width, reach, pieces=(), kind=jnp.bfloat16):
    level = level_of(rng, shape, pieces, -0.22, 0.18) if pieces else 1.0
    result = jax.random.normal(rng, shape, jnp.float32) * width * level
    return jnp.minimum(jnp.maximum(result, -reach), reach).astype(kind)


def setup_inputs(seed: int = 0) -> dict:
    seeds = jax.random.split(jax.random.key(seed), 11)
    hidden = gaussian(seeds[0], (LAYERS, SAMPLES * TXT, D), 1.0, 6.0, ((0, 8), (1, 4), (2, 32)))
    q_weight = gaussian(seeds[1], (LAYERS, D, H * HD), D ** -0.5, 0.0625, ((0, 8), (2, 32)))
    o_weight = gaussian(seeds[2], (LAYERS, H * HD, D), (H * HD) ** -0.5, 0.0625, ((0, 8), (1, 32)))
    vision_kv = gaussian(seeds[3], (LAYERS, SAMPLES, VIS, 2 * KVH * HD), 1.0, 6.0, ((2, 1024),))
    q_gain = draw_q_gain(jax.random.fold_in(seeds[10], 71), 0)
    k_gain = draw_k_gain(jax.random.fold_in(seeds[10], 71), 0)
    attn_gate = jnp.clip(0.25 + 1.25 * jax.random.uniform(seeds[6], (LAYERS,), jnp.float32) ** level_of(seeds[6], (LAYERS,), ((0, 8),), -0.2, 0.2), 0.25, 1.5)
    images = touch_ends(jax.random.randint(seeds[7], (SAMPLES,), 1, IMG + 1), jax.random.fold_in(seeds[7], 1), 1, IMG).astype(jnp.int32)
    tiles = touch_ends(jax.random.randint(seeds[8], (SAMPLES, IMG), 1, TILES + 1), jax.random.fold_in(seeds[8], 1), 1, TILES).astype(jnp.int32)
    text_start = touch_ends(jax.random.randint(seeds[9], (SAMPLES, IMG), 0, TXT), jax.random.fold_in(seeds[9], 1), 0, TXT - 1).astype(jnp.int32)
    return dict(hidden=hidden, q_weight=q_weight, o_weight=o_weight, vision_kv=vision_kv, q_gain=q_gain, k_gain=k_gain, attn_gate=attn_gate, images=images, tiles=tiles, text_start=text_start)


def normalize(values, gain):
    mean_square = lax.optimization_barrier(jnp.mean(values * values, axis=-1, keepdims=True))
    return values * lax.rsqrt(mean_square + 1e-05) * gain

def key_mask(images, tiles, text_start, position):
    image_of = position // (TILES * P_SIZE)
    tile_of = position // P_SIZE % TILES
    onehot = (image_of[None, :] == jnp.arange(IMG, dtype=jnp.int32)[:, None]).astype(jnp.int32)
    tile_limit = lax.optimization_barrier(jnp.sum(tiles[:, :, None] * onehot[None], axis=1))
    first_row = lax.optimization_barrier(jnp.sum(text_start[:, :, None] * onehot[None], axis=1))
    live = (image_of[None, :] < images[:, None]) & (tile_of[None, :] < tile_limit)
    text_rows = jnp.arange(TXT, dtype=jnp.int32)
    return live[:, None, :] & (text_rows[None, :, None] >= first_row[:, None, :])

def masked_softmax(scores, mask):
    top = lax.optimization_barrier(jnp.max(jnp.where(mask, scores, -1e+30), axis=-1, keepdims=True))
    expo = jnp.where(mask, jnp.exp(scores - top), 0.0)
    total = jnp.maximum(lax.optimization_barrier(jnp.sum(expo, axis=-1, keepdims=True)), 1.0)
    return (expo / total).astype(jnp.bfloat16)

def reference(hidden, q_weight, o_weight, vision_kv, q_gain, k_gain, attn_gate, images, tiles, text_start):
    groups = H // KVH
    position = jnp.arange(VIS, dtype=jnp.int32)
    mask = key_mask(images, tiles, text_start, position)
    outputs = []
    for layer in range(LAYERS):
        text_in = hidden[layer]
        queries = jnp.dot(text_in, q_weight[layer], preferred_element_type=jnp.float32)
        queries = normalize(queries.reshape(SAMPLES, TXT, KVH, groups, HD), q_gain[layer]).astype(jnp.bfloat16)
        pairs = vision_kv[layer].reshape(SAMPLES, VIS, KVH, 2, HD)
        keys = normalize(pairs[:, :, :, 0, :].astype(jnp.float32), k_gain[layer]).astype(jnp.bfloat16)
        values = pairs[:, :, :, 1, :]
        scores = jnp.einsum('stkgd,svkd->skgtv', queries.astype(jnp.float32), keys.astype(jnp.float32)) * HD ** (-0.5)
        weights = masked_softmax(scores, mask[:, None, None])
        mixed = jnp.einsum('skgtv,svkd->stkgd', weights.astype(jnp.float32), values.astype(jnp.float32)).astype(jnp.bfloat16)
        branch = jnp.dot(mixed.reshape(SAMPLES * TXT, H * HD), o_weight[layer], preferred_element_type=jnp.float32)
        outputs.append((text_in.astype(jnp.float32) + jnp.tanh(attn_gate[layer]) * branch).astype(jnp.bfloat16))
    return jnp.stack(outputs)
```

```python
import functools

import jax
import jax.numpy as jnp
from jax import lax
from jax.experimental import pallas as pl
from jax.experimental.pallas import tpu as pltpu
from jax.sharding import PartitionSpec as P

TILES = 4
P_SIZE = 128
MESH = pl.DeviceIdType.MESH
BEFORE_KV = 4


def kernel(
    sizes,
    hidden_ref, kv_ref, qw_hbm, ow_hbm, q_gain_ref, k_gain_ref, gate_ref, images_ref, tiles_ref, start_ref,
    out_ref,
    hid_all, qw, ow, acc, kvx, kv_all, keys, queries, limits, scores, weights, mixed, part,
    got_r, got_l, put_r, put_l,
    local_sem, ag_recv, ag_send_r, ag_send_l, x_recv, x_send, z_recv, z_send, own_send, chain_r, chain_l,
    rs_recv_r, rs_recv_l, rs_send_r, rs_send_l,
):
    n_replica, n_section, n_tensor, kv_heads = sizes
    plane = n_replica * n_section
    group = n_tensor // kv_heads
    reach = (n_tensor - group) // 2
    turn = n_tensor // 2
    rows, width = hidden_ref.shape
    half = rows // 2
    head_dim = width // 2
    block = 2 * plane
    dp = lax.axis_index("dp")
    sec = lax.axis_index("section")
    t = lax.axis_index("tensor")
    me = dp * n_section + sec
    mine = t // group
    j = t % group
    base = mine * group

    def ring(offset):
        return (t + offset + n_tensor) % n_tensor

    right = ring(1)
    left = ring(-1)

    def z_dev(index):
        return (dp, sec, index)

    def plane_dev(index):
        return (index // n_section, index % n_section, t)

    barrier = pltpu.get_barrier_semaphore()

    @pl.loop(1, plane)
    def _(p):
        pl.semaphore_signal(barrier, inc=1, device_id=plane_dev((me + p) % plane), device_id_type=MESH)

    @pl.loop(1, reach + 1)
    def _(p):
        pl.semaphore_signal(barrier, inc=1, device_id=z_dev(ring(p)), device_id_type=MESH)
        pl.semaphore_signal(barrier, inc=1, device_id=z_dev(ring(-p)), device_id_type=MESH)

    qw_copy = pltpu.make_async_copy(qw_hbm, qw, local_sem.at[0])
    ow_copy = pltpu.make_async_copy(ow_hbm, ow, local_sem.at[1])
    qw_copy.start()
    ow_copy.start()
    pl.semaphore_wait(barrier, plane - 1 + 2 * reach)

    def ag_copy(src_ref, source, b, sem, target):
        return pltpu.make_async_remote_copy(
            src_ref=src_ref, dst_ref=hid_all.at[source, b], send_sem=sem, recv_sem=ag_recv.at[source, b],
            device_id=z_dev(target), device_id_type=MESH,
        )

    for b in range(2):
        piece = hidden_ref.at[pl.ds(b * half, half)]
        ag_copy(piece, t, b, ag_send_r.at[0, b], right).start()
        ag_copy(piece, t, b, ag_send_l.at[0, b], left).start()

    def x_copy(peer):
        return pltpu.make_async_remote_copy(
            src_ref=kv_ref.at[peer % n_section, peer // n_section],
            dst_ref=kvx.at[:, pl.ds(2 * me, 2)],
            send_sem=x_send.at[peer], recv_sem=x_recv.at[me],
            device_id=plane_dev(peer), device_id_type=MESH,
        )

    def x_arrival(peer):
        return pltpu.make_async_remote_copy(
            src_ref=kv_ref.at[peer % n_section, peer // n_section],
            dst_ref=kvx.at[:, pl.ds(2 * peer, 2)],
            send_sem=x_send.at[peer], recv_sem=x_recv.at[peer],
            device_id=plane_dev(peer), device_id_type=MESH,
        )

    @pl.loop(1, plane)
    def _(p):
        x_copy((me + p) % plane).start()

    own_x = pltpu.make_async_copy(kv_ref.at[sec, dp], kvx.at[:, pl.ds(2 * me, 2)], local_sem.at[2])
    own_x.start()

    qw_copy.wait()
    acc[...] = jnp.dot(
        hidden_ref[...], qw[pl.ds(pl.multiple_of(t * width, width), width), :], preferred_element_type=jnp.float32
    )

    def project(source):
        chunk = hid_all[source].reshape(rows, width)
        acc[...] += jnp.dot(
            chunk, qw[pl.ds(pl.multiple_of(source * width, width), width), :], preferred_element_type=jnp.float32
        )

    def ag_step(k, carry):
        from_left = ring(-k)
        from_right = ring(k)
        for b in range(2):
            ag_copy(hid_all.at[from_left, b], from_left, b, ag_send_r.at[k, b], right).wait_recv()
            ag_copy(hid_all.at[from_left, b], from_left, b, ag_send_r.at[k, b], right).start()
            ag_copy(hid_all.at[from_right, b], from_right, b, ag_send_l.at[k, b], left).wait_recv()
            ag_copy(hid_all.at[from_right, b], from_right, b, ag_send_l.at[k, b], left).start()
        project(from_left)
        project(from_right)
        return carry

    lax.fori_loop(1, BEFORE_KV, ag_step, 0)

    def z_copy(head, source_ref, source, sem, target):
        del head
        return pltpu.make_async_remote_copy(
            src_ref=source_ref, dst_ref=kv_all.at[source], send_sem=sem, recv_sem=z_recv.at[source],
            device_id=z_dev(target), device_id_type=MESH,
        )

    @pl.loop(1, plane)
    def _(p):
        x_arrival((me + p) % plane).wait_recv()

    own_x.wait()

    def entry(i):
        head = (mine + i) % kv_heads
        ahead = (group * head - t + n_tensor) % n_tensor
        target = group * head + (group - 1) * (ahead // (reach + 1))
        return z_copy(head, kvx.at[pl.ds(2 * head, 2)], t, z_send.at[i], target)

    @pl.loop(1, kv_heads)
    def _(i):
        entry(i).start()

    own_block = kvx.at[pl.ds(2 * mine, 2)]
    own_right = z_copy(mine, own_block, t, own_send.at[0], right)
    own_left = z_copy(mine, own_block, t, own_send.at[1], left)

    @pl.when(j < group - 1)
    def _():
        own_right.start()

    @pl.when(j > 0)
    def _():
        own_left.start()

    own_z = pltpu.make_async_copy(own_block, kv_all.at[t], local_sem.at[3])
    own_z.start()

    lax.fori_loop(BEFORE_KV, turn - 1, ag_step, 0)

    def ag_last(k, to_right, to_left):
        for b in range(2):
            if to_right[b] is not None:
                src = ring(-k)
                ag_copy(hid_all.at[src, b], src, b, ag_send_r.at[k % turn, b], right).wait_recv()
                if to_right[b]:
                    ag_copy(hid_all.at[src, b], src, b, ag_send_r.at[k, b], right).start()
            if to_left[b] is not None:
                src = ring(k)
                ag_copy(hid_all.at[src, b], src, b, ag_send_l.at[k % turn, b], left).wait_recv()
                if to_left[b]:
                    ag_copy(hid_all.at[src, b], src, b, ag_send_l.at[k, b], left).start()

    ag_last(turn - 1, (True, False), (False, True))
    project(ring(1 - turn))
    project(ring(turn - 1))
    ag_last(turn, (False, None), (None, False))
    project(ring(turn))

    for h in range(2):
        raw = acc[:, h * head_dim : (h + 1) * head_dim]
        square = jnp.mean(raw * raw, axis=-1, keepdims=True)
        queries[h * rows : (h + 1) * rows, :] = (raw * lax.rsqrt(square + 1e-05) * q_gain_ref[...]).astype(jnp.bfloat16)

    slots = n_tensor * block
    column = lax.broadcasted_iota(jnp.int32, (1, slots), 1)
    position = (column % block) // 2 * n_tensor + column // block
    image_of = position // (TILES * P_SIZE)
    tile_of = position // P_SIZE % TILES
    for m in range(2):
        sample = dp * 2 + m
        limit = jnp.full((1, slots), half, jnp.int32)
        for image in range(tiles_ref.shape[1]):
            fits = (image_of == image) & (tile_of < tiles_ref[sample, image]) & (image < images_ref[sample])
            limit = jnp.where(fits, start_ref[sample, image], limit)
        limits[m] = jnp.where(column % 2 == m, limit, half)

    def take(source):
        raw = kv_all[source, 0].astype(jnp.float32)
        square = jnp.mean(raw * raw, axis=-1, keepdims=True)
        keys[source] = (raw * lax.rsqrt(square + 1e-05) * k_gain_ref[...]).astype(jnp.bfloat16)

    own_z.wait()
    take(t)

    def chain(n, carry):
        @pl.when(n < reach + j)
        def _():
            src = ring(-1 - n)
            z_copy(mine, kv_all.at[src], src, chain_r.at[n], right).wait_recv()

            @pl.when(j < group - 1)
            def _():
                z_copy(mine, kv_all.at[src], src, chain_r.at[n], right).start()

        @pl.when(n < reach + group - 1 - j)
        def _():
            src = ring(1 + n)
            z_copy(mine, kv_all.at[src], src, chain_l.at[n], left).wait_recv()

            @pl.when(j > 0)
            def _():
                z_copy(mine, kv_all.at[src], src, chain_l.at[n], left).start()

        @pl.when(n < reach + j)
        def _():
            take(ring(-1 - n))

        @pl.when(n < reach + group - 1 - j)
        def _():
            take(ring(1 + n))

        return carry

    lax.fori_loop(0, reach + group - 1, chain, 0)

    scores[...] = lax.dot_general(
        queries[...], keys[...].reshape(slots, head_dim), (((1,), (1,)), ((), ())), preferred_element_type=jnp.float32
    ) * head_dim ** (-0.5)
    step_rows = 16 if half % 16 == 0 else half

    def soften(i, carry):
        r0 = pl.multiple_of(i * step_rows, step_rows)
        m = r0 // half % 2
        text_row = r0 % half + lax.broadcasted_iota(jnp.int32, (step_rows, slots), 0)
        seen = text_row >= limits[m]
        found = jnp.where(seen, scores[pl.ds(r0, step_rows), :], -1e30)
        top = jnp.max(found, axis=-1, keepdims=True)
        expo = jnp.where(seen, jnp.exp(found - top), 0.0)
        total = jnp.maximum(jnp.sum(expo, axis=-1, keepdims=True), 1.0)
        weights[pl.ds(r0, step_rows), :] = (expo / total).astype(jnp.bfloat16)
        return carry

    lax.fori_loop(0, 2 * rows // step_rows, soften, 0)
    both = jnp.dot(
        weights[...], kv_all[:, 1].reshape(slots, head_dim), preferred_element_type=jnp.float32
    ).astype(jnp.bfloat16)
    mixed[:, :head_dim] = both[:rows]
    mixed[:, head_dim:] = both[rows:]

    def share(dest):
        return jnp.dot(
            mixed[...], ow[:, pl.ds(pl.multiple_of(dest * width, width), width)], preferred_element_type=jnp.float32
        )

    def rs_copy(put, got, send, recv, k, b, target):
        return pltpu.make_async_remote_copy(
            src_ref=put.at[k, b], dst_ref=got.at[k, b], send_sem=send.at[k, b], recv_sem=recv.at[k, b],
            device_id=z_dev(target), device_id_type=MESH,
        )

    go_right = functools.partial(rs_copy, put_r, got_r, rs_send_r, rs_recv_r)
    go_left = functools.partial(rs_copy, put_l, got_l, rs_send_l, rs_recv_l)

    ow_copy.wait()
    part[0] = share(ring(turn))
    part[1] = share(ring(1 - turn))
    for b in range(2):
        span = slice(b * half, (b + 1) * half)
        put_r[0, b] = part[0, span].astype(jnp.bfloat16)
        go_right(0, b, right).start()
        put_l[0, b] = part[1, span].astype(jnp.bfloat16)
        go_left(0, b, left).start()
    part[0] = share(ring(turn - 1))
    part[1] = share(ring(2 - turn))

    def rs_step(k, carry):
        for b in range(2):
            span = slice(b * half, (b + 1) * half)
            go_right(k - 1, b, right).wait_recv()
            put_r[k, b] = (got_r[k - 1, b].astype(jnp.float32) + part[0, span]).astype(jnp.bfloat16)
            go_right(k, b, right).start()
            go_left(k - 1, b, left).wait_recv()
            put_l[k, b] = (got_l[k - 1, b].astype(jnp.float32) + part[1, span]).astype(jnp.bfloat16)
            go_left(k, b, left).start()
        part[0] = share(ring(turn - 1 - k))
        part[1] = share(ring(k + 2 - turn))
        return carry

    lax.fori_loop(1, turn - 1, rs_step, 0)
    last = turn - 1
    scale = jnp.tanh(jnp.full((1, width), gate_ref[0], jnp.float32))
    for b in range(2):
        span = slice(b * half, (b + 1) * half)
        go_right(last - 1, b, right).wait_recv()
        put_r[last, b] = (got_r[last - 1, b].astype(jnp.float32) + part[0, span]).astype(jnp.bfloat16)
        go_right(last, b, right).start()
    for b in range(2):
        span = slice(b * half, (b + 1) * half)
        go_left(last - 1, b, left).wait_recv()
        part[1, span] += got_l[last - 1, b].astype(jnp.float32)
    for b in range(2):
        span = slice(b * half, (b + 1) * half)
        go_right(last, b, right).wait_recv()
        total = part[1, span] + got_r[last, b].astype(jnp.float32)
        out_ref[span, :] = (hidden_ref[span, :].astype(jnp.float32) + scale * total).astype(jnp.bfloat16)

    @pl.loop(0, turn - 1)
    def _(k):
        for b in range(2):
            ag_copy(hid_all.at[0, b], 0, b, ag_send_r.at[k, b], right).wait_send()
            ag_copy(hid_all.at[0, b], 0, b, ag_send_l.at[k, b], left).wait_send()

    ag_copy(hid_all.at[0, 0], 0, 0, ag_send_r.at[turn - 1, 0], right).wait_send()
    ag_copy(hid_all.at[0, 1], 0, 1, ag_send_l.at[turn - 1, 1], left).wait_send()

    @pl.loop(1, plane)
    def _(p):
        x_copy((me + p) % plane).wait_send()

    @pl.loop(1, kv_heads)
    def _(i):
        entry(i).wait_send()

    @pl.when(j < group - 1)
    def _():
        own_right.wait_send()

        @pl.loop(0, reach + j)
        def _(n):
            z_copy(mine, kv_all.at[0], 0, chain_r.at[n], right).wait_send()

    @pl.when(j > 0)
    def _():
        own_left.wait_send()

        @pl.loop(0, reach + group - 1 - j)
        def _(n):
            z_copy(mine, kv_all.at[0], 0, chain_l.at[n], left).wait_send()

    @pl.loop(0, turn - 1)
    def _(k):
        for b in range(2):
            go_right(k, b, right).wait_send()
            go_left(k, b, left).wait_send()

    for b in range(2):
        go_right(last, b, right).wait_send()


def on_device(
    hidden, q_weight, o_weight, vision_kv, q_gain, k_gain, attn_gate, images, tiles, text_start
):
    n_tensor = lax.axis_size("tensor")
    n_section = lax.axis_size("section")
    n_replica = lax.axis_size("dp")
    plane = n_section * n_replica
    head_dim = q_gain.shape[1]
    kv_heads = vision_kv.shape[3] // (2 * head_dim)
    rows, width = hidden.shape[1:]
    half = rows // 2
    turn = n_tensor // 2
    group = n_tensor // kv_heads
    reach = (n_tensor - group) // 2
    slots = n_tensor * 2 * plane
    kv = vision_kv.reshape(n_section, n_replica, 2, 2 * kv_heads, head_dim).swapaxes(2, 3)
    bf16, f32 = jnp.bfloat16, jnp.float32
    dma = pltpu.SemaphoreType.DMA
    vmem = pl.BlockSpec(memory_space=pltpu.VMEM)
    smem = pl.BlockSpec(memory_space=pltpu.SMEM)
    hbm = pl.BlockSpec(memory_space=pl.ANY)
    out = pl.pallas_call(
        functools.partial(kernel, (n_replica, n_section, n_tensor, kv_heads)),
        out_shape=jax.ShapeDtypeStruct((rows, width), bf16),
        in_specs=[vmem, vmem, hbm, hbm, vmem, vmem, smem, smem, smem, smem],
        out_specs=vmem,
        scratch_shapes=[
            pltpu.VMEM((n_tensor, 2, half, width), bf16),
            pltpu.VMEM(q_weight.shape[1:], bf16),
            pltpu.VMEM(o_weight.shape[1:], bf16),
            pltpu.VMEM((rows, width), f32),
            pltpu.VMEM((2 * kv_heads, 2 * plane, head_dim), bf16),
            pltpu.VMEM((n_tensor, 2, 2 * plane, head_dim), bf16),
            pltpu.VMEM((n_tensor, 2 * plane, head_dim), bf16),
            pltpu.VMEM((2 * rows, head_dim), bf16),
            pltpu.VMEM((2, 1, slots), jnp.int32),
            pltpu.VMEM((2 * rows, slots), f32),
            pltpu.VMEM((2 * rows, slots), bf16),
            pltpu.VMEM((rows, width), bf16),
            pltpu.VMEM((2, rows, width), f32),
            pltpu.VMEM((turn, 2, half, width), bf16),
            pltpu.VMEM((turn - 1, 2, half, width), bf16),
            pltpu.VMEM((turn, 2, half, width), bf16),
            pltpu.VMEM((turn - 1, 2, half, width), bf16),
            dma((4,)),
            dma((n_tensor, 2)),
            dma((turn, 2)),
            dma((turn, 2)),
            dma((plane,)),
            dma((plane,)),
            dma((n_tensor,)),
            dma((kv_heads,)),
            dma((2,)),
            dma((reach + group - 1,)),
            dma((reach + group - 1,)),
            dma((turn, 2)),
            dma((turn - 1, 2)),
            dma((turn, 2)),
            dma((turn - 1, 2)),
        ],
        compiler_params=pltpu.CompilerParams(
            collective_id=0, has_side_effects=True, vmem_limit_bytes=48 * 1024 * 1024
        ),
    )(
        hidden[0], kv, q_weight[0], o_weight[0], q_gain, k_gain, attn_gate, images, tiles, text_start
    )
    return out[None]


def solution(mesh):
    return jax.shard_map(
        on_device,
        mesh=mesh,
        in_specs=(
            P("section", "dp", "tensor"),
            P("section", None, "tensor"),
            P("section", "tensor", None),
            P(None, None, ("dp", "section", "tensor"), None),
            P("section", None),
            P("section", None),
            P("section"),
            P(),
            P(),
            P(),
        ),
        out_specs=P("section", "dp", "tensor"),
        check_vma=False,
    )
```

```python
import functools

import jax
import jax.numpy as jnp
from jax import lax
from jax.experimental import pallas as pl
from jax.experimental.pallas import tpu as pltpu
from jax.sharding import PartitionSpec as P

TILES = 4
P_SIZE = 128
MESH = pl.DeviceIdType.MESH
EXCHANGED = 3
CHAINED = 6


def kernel(
    sizes,
    hidden_hbm, kv_hbm, qw_hbm, ow_hbm, q_gain_hbm, k_gain_hbm, gate_hbm, images_hbm, tiles_hbm, start_hbm,
    out_ref,
    hid_all, kv_own, qw, ow, q_gain, k_gain, gate, images, tiles, start,
    acc, kvx, kv_all, keys, queries, limits, scores, weights, mixed, part,
    got_r, got_l, put_r, put_l,
    local_sem, kv_sem, ag_recv, ag_send_r, ag_send_l, x_recv, x_send, z_recv, z_send, own_send, chain_r, chain_l,
    rs_recv_r, rs_recv_l, rs_send_r, rs_send_l,
):
    n_replica, n_section, n_tensor, kv_heads = sizes
    plane = n_replica * n_section
    group = n_tensor // kv_heads
    reach = (n_tensor - group) // 2
    turn = n_tensor // 2
    last = turn - 1
    links = reach + group - 1
    rows, width = out_ref.shape
    half = rows // 2
    head_dim = width // 2
    block = 2 * plane
    slots = n_tensor * block
    dp = lax.axis_index("dp")
    sec = lax.axis_index("section")
    t = lax.axis_index("tensor")
    me = dp * n_section + sec
    mine = t // group
    j = t % group

    def ring(offset):
        return (t + offset + n_tensor) % n_tensor

    right = ring(1)
    left = ring(-1)

    def z_dev(index):
        return (dp, sec, index)

    def plane_dev(index):
        return (index // n_section, index % n_section, t)

    barrier = pltpu.get_barrier_semaphore()

    @pl.loop(0, reach)
    def _(p):
        pl.semaphore_signal(barrier, inc=1, device_id=z_dev(ring(reach - p)), device_id_type=MESH)
        pl.semaphore_signal(barrier, inc=1, device_id=z_dev(ring(p - reach)), device_id_type=MESH)

    @pl.loop(1, plane)
    def _(p):
        pl.semaphore_signal(barrier, inc=1, device_id=plane_dev((me + p) % plane), device_id_type=MESH)

    local = [
        pltpu.make_async_copy(src, dst, local_sem.at[i])
        for i, (src, dst) in enumerate([
            (hidden_hbm.at[pl.ds(0, half)], hid_all.at[t, 0]),
            (hidden_hbm.at[pl.ds(half, half)], hid_all.at[t, 1]),
            (qw_hbm, qw),
            (images_hbm, images),
            (tiles_hbm, tiles),
            (start_hbm, start),
            (q_gain_hbm, q_gain),
            (k_gain_hbm, k_gain),
            (gate_hbm, gate),
            (ow_hbm, ow),
        ])
    ]
    columns = [
        pltpu.make_async_copy(
            kv_hbm.at[:, :, pl.ds(i * head_dim, head_dim)], kv_own.at[i], kv_sem.at[i]
        )
        for i in range(2 * kv_heads)
    ]
    for copy in local[:2] + columns + local[2:]:
        copy.start()
    acc[...] = jnp.zeros_like(acc)
    for copy in local[:2] + columns + local[2:]:
        copy.wait()
    pl.semaphore_wait(barrier, plane - 1 + 2 * reach)

    def ag_copy(source, b, sem, target):
        piece = hid_all.at[source, b]
        return pltpu.make_async_remote_copy(
            src_ref=piece, dst_ref=piece, send_sem=sem, recv_sem=ag_recv.at[source, b],
            device_id=z_dev(target), device_id_type=MESH,
        )

    def ag_right(k, b):
        return ag_copy(ring(-k), b, ag_send_r.at[k % turn, b], right)

    def ag_left(k, b):
        return ag_copy(ring(k), b, ag_send_l.at[k % turn, b], left)

    def x_copy(peer, origin):
        return pltpu.make_async_remote_copy(
            src_ref=kv_own.at[:, peer % n_section, pl.ds(2 * (peer // n_section), 2)],
            dst_ref=kvx.at[:, pl.ds(2 * origin, 2)],
            send_sem=x_send.at[peer], recv_sem=x_recv.at[origin],
            device_id=plane_dev(peer), device_id_type=MESH,
        )

    ag_right(0, 0).start()
    ag_left(0, 0).start()

    @pl.loop(1, plane)
    def _(p):
        x_copy((me + p) % plane, me).start()

    own_x = pltpu.make_async_copy(
        kv_own.at[:, sec, pl.ds(2 * dp, 2)], kvx.at[:, pl.ds(2 * me, 2)], local_sem.at[10]
    )
    own_x.start()
    ag_right(0, 1).start()
    ag_left(0, 1).start()

    column = lax.broadcasted_iota(jnp.int32, (1, slots), 1)
    position = (column % block) // 2 * n_tensor + column // block
    image_of = position // (TILES * P_SIZE)
    tile_of = position // P_SIZE % TILES
    for m in range(2):
        sample = dp * 2 + m
        limit = jnp.full((1, slots), half, jnp.int32)
        for image in range(tiles.shape[0]):
            fits = (image_of == image) & (tile_of < tiles[image, sample]) & (image < images[sample])
            limit = jnp.where(fits, start[image, sample], limit)
        limits[m] = jnp.where(column % 2 == m, limit, half)

    def z_copy(source_ref, source, sem, target):
        return pltpu.make_async_remote_copy(
            src_ref=source_ref, dst_ref=kv_all.at[source], send_sem=sem, recv_sem=z_recv.at[source],
            device_id=z_dev(target), device_id_type=MESH,
        )

    def entry(i):
        head = (mine + i) % kv_heads
        ahead = (group * head - t + n_tensor) % n_tensor
        target = group * head + (group - 1) * (ahead // (reach + 1))
        return z_copy(kvx.at[pl.ds(2 * head, 2)], t, z_send.at[i], target)

    def pass_right(n):
        src = ring(-1 - n)
        return z_copy(kv_all.at[src], src, chain_r.at[n], right)

    def pass_left(n):
        src = ring(1 + n)
        return z_copy(kv_all.at[src], src, chain_l.at[n], left)

    own_block = kvx.at[pl.ds(2 * mine, 2)]
    own_right = z_copy(own_block, t, own_send.at[0], right)
    own_left = z_copy(own_block, t, own_send.at[1], left)
    own_z = pltpu.make_async_copy(own_block, kv_all.at[t], local_sem.at[11])

    def take(source):
        raw = kv_all[source, 0].astype(jnp.float32)
        square = jnp.mean(raw * raw, axis=-1, keepdims=True)
        keys[source] = (raw * lax.rsqrt(square + 1e-05) * k_gain[...]).astype(jnp.bfloat16)

    def chain(n):
        to_left_end = n < reach + j
        to_right_end = n < links - j

        @pl.when(to_left_end)
        def _():
            pass_right(n).wait_recv()

            @pl.when(j < group - 1)
            def _():
                pass_right(n).start()

        @pl.when(to_right_end)
        def _():
            pass_left(n).wait_recv()

            @pl.when(j > 0)
            def _():
                pass_left(n).start()

        @pl.when(to_left_end)
        def _():
            take(ring(-1 - n))

        @pl.when(to_right_end)
        def _():
            take(ring(1 + n))

    def enter(q):
        entry(q).start()

        @pl.when(2 * q != kv_heads)
        def _():
            entry(kv_heads - q).start()

    def project(source):
        chunk = hid_all[source].reshape(rows, width)
        acc[...] += jnp.dot(
            chunk, qw[pl.ds(pl.multiple_of(source * width, width), width), :], preferred_element_type=jnp.float32
        )

    def ag_step(k, carry):
        ag_right(k, 0).wait_recv()
        ag_right(k, 0).start()
        ag_left(k, 0).wait_recv()
        ag_left(k, 0).start()
        project(ring(1 - k))

        @pl.when(k == EXCHANGED)
        def _():
            @pl.loop(1, plane)
            def _(p):
                peer = (me + p) % plane
                x_copy(peer, peer).wait_recv()

            own_x.wait()
            own_z.start()

            @pl.when(j < group - 1)
            def _():
                own_right.start()

            @pl.when(j > 0)
            def _():
                own_left.start()

        ag_right(k, 1).wait_recv()
        ag_right(k, 1).start()
        ag_left(k, 1).wait_recv()
        ag_left(k, 1).start()

        @pl.when((k >= EXCHANGED) & ((k - EXCHANGED) % 2 == 0) & (k < EXCHANGED + kv_heads))
        def _():
            enter((k - EXCHANGED) // 2 + 1)

        @pl.when(k > 1)
        def _():
            project(ring(k - 1))

        @pl.when(k >= CHAINED)
        def _():
            for n in range(2):
                @pl.when(2 * (k - CHAINED) + n < links)
                def _():
                    chain(2 * (k - CHAINED) + n)

        return carry

    lax.fori_loop(1, last, ag_step, 0)

    ag_right(last, 0).wait_recv()
    ag_right(last, 0).start()
    ag_left(last, 1).wait_recv()
    ag_left(last, 1).start()
    project(ring(1 - last))
    project(ring(last - 1))
    ag_right(last, 1).wait_recv()
    ag_left(last, 0).wait_recv()
    project(ring(-last))
    project(ring(last))

    @pl.loop(2 * max(0, last - CHAINED), links)
    def _(n):
        chain(n)

    own_z.wait()
    take(t)
    ag_right(turn, 0).wait_recv()
    ag_left(turn, 1).wait_recv()
    project(ring(turn))

    for h in range(2):
        raw = acc[:, h * head_dim : (h + 1) * head_dim]
        square = jnp.mean(raw * raw, axis=-1, keepdims=True)
        normal = (raw * lax.rsqrt(square + 1e-05) * q_gain[...]).astype(jnp.bfloat16)
        for m in range(2):
            queries[m, h * half : (h + 1) * half, :] = normal[m * half : (m + 1) * half]

    step_rows = 16 if half % 16 == 0 else half

    def attend(m):
        scores[...] = lax.dot_general(
            queries[m], keys[...].reshape(slots, head_dim), (((1,), (1,)), ((), ())),
            preferred_element_type=jnp.float32,
        ) * head_dim ** (-0.5)

        def soften(i, carry):
            r0 = pl.multiple_of(i * step_rows, step_rows)
            text_row = r0 % half + lax.broadcasted_iota(jnp.int32, (step_rows, slots), 0)
            seen = text_row >= limits[m]
            found = jnp.where(seen, scores[pl.ds(r0, step_rows), :], -1e30)
            top = jnp.max(found, axis=-1, keepdims=True)
            expo = jnp.where(seen, jnp.exp(found - top), 0.0)
            total = jnp.maximum(jnp.sum(expo, axis=-1, keepdims=True), 1.0)
            weights[pl.ds(r0, step_rows), :] = (expo / total).astype(jnp.bfloat16)
            return carry

        lax.fori_loop(0, rows // step_rows, soften, 0)
        both = jnp.dot(
            weights[...], kv_all[:, 1].reshape(slots, head_dim), preferred_element_type=jnp.float32
        ).astype(jnp.bfloat16)
        for h in range(2):
            mixed[m * half : (m + 1) * half, h * head_dim : (h + 1) * head_dim] = both[h * half : (h + 1) * half]

    def share(dest, span):
        return jnp.dot(
            mixed[span, :], ow[:, pl.ds(pl.multiple_of(dest * width, width), width)],
            preferred_element_type=jnp.float32,
        )

    def rs_copy(put, got, send, recv, target, k, b):
        return pltpu.make_async_remote_copy(
            src_ref=put.at[k, b], dst_ref=got.at[k, b], send_sem=send.at[k, b], recv_sem=recv.at[k, b],
            device_id=z_dev(target), device_id_type=MESH,
        )

    go_right = functools.partial(rs_copy, put_r, got_r, rs_send_r, rs_recv_r, right)
    go_left = functools.partial(rs_copy, put_l, got_l, rs_send_l, rs_recv_l, left)
    spans = (slice(0, half), slice(half, rows))
    whole = slice(0, rows)

    for b in range(2):
        attend(b)
        put_r[0, b] = share(ring(turn), spans[b]).astype(jnp.bfloat16)
        go_right(0, b).start()
        put_l[0, b] = share(ring(1 - turn), spans[b]).astype(jnp.bfloat16)
        go_left(0, b).start()
    part[1, 0] = share(ring(turn - 1), whole)
    part[1, 1] = share(ring(2 - turn), whole)

    def sum_right(k, b):
        go_right(k - 1, b).wait_recv()
        put_r[k, b] = (got_r[k - 1, b].astype(jnp.float32) + part[k % 2, 0, spans[b]]).astype(jnp.bfloat16)
        go_right(k, b).start()

    def sum_left(k, b):
        go_left(k - 1, b).wait_recv()
        put_l[k, b] = (got_l[k - 1, b].astype(jnp.float32) + part[k % 2, 1, spans[b]]).astype(jnp.bfloat16)
        go_left(k, b).start()

    def rs_step(k, carry):
        sum_right(k, 0)
        sum_left(k, 0)
        part[(k + 1) % 2, 0] = share(ring(turn - 1 - k), whole)
        sum_right(k, 1)
        sum_left(k, 1)
        part[(k + 1) % 2, 1] = share(ring(k + 2 - turn), whole)
        for b in range(2):
            ag_right(k - 1, b).wait_send()
            ag_left(k - 1, b).wait_send()
            go_right(k - 1, b).wait_send()
            go_left(k - 1, b).wait_send()
        return carry

    lax.fori_loop(1, last, rs_step, 0)
    sum_right(last, 0)
    sum_right(last, 1)

    for b in range(2):
        ag_right(last - 1, b).wait_send()
        ag_left(last - 1, b).wait_send()
        go_right(last - 1, b).wait_send()
        go_left(last - 1, b).wait_send()
    ag_right(last, 0).wait_send()
    ag_left(last, 1).wait_send()

    @pl.loop(1, plane)
    def _(p):
        x_copy((me + p) % plane, me).wait_send()

    @pl.loop(1, kv_heads)
    def _(i):
        entry(i).wait_send()

    @pl.when(j < group - 1)
    def _():
        own_right.wait_send()

        @pl.loop(0, reach + j)
        def _(n):
            pass_right(n).wait_send()

    @pl.when(j > 0)
    def _():
        own_left.wait_send()

        @pl.loop(0, links - j)
        def _(n):
            pass_left(n).wait_send()

    scale = jnp.tanh(jnp.full((1, width), gate[0], jnp.float32))
    for b in range(2):
        go_left(last - 1, b).wait_recv()
        go_right(last, b).wait_recv()
        total = part[last % 2, 1, spans[b]] + got_l[last - 1, b].astype(jnp.float32) + got_r[last, b].astype(jnp.float32)
        out_ref[spans[b], :] = (hid_all[t, b].astype(jnp.float32) + scale * total).astype(jnp.bfloat16)
    for b in range(2):
        go_right(last, b).wait_send()


def on_device(
    hidden, q_weight, o_weight, vision_kv, q_gain, k_gain, attn_gate, images, tiles, text_start
):
    n_tensor = lax.axis_size("tensor")
    n_section = lax.axis_size("section")
    n_replica = lax.axis_size("dp")
    plane = n_section * n_replica
    head_dim = q_gain.shape[1]
    kv_heads = vision_kv.shape[3] // (2 * head_dim)
    rows, width = hidden.shape[1:]
    half = rows // 2
    turn = n_tensor // 2
    group = n_tensor // kv_heads
    reach = (n_tensor - group) // 2
    slots = n_tensor * 2 * plane
    bf16, f32, i32 = jnp.bfloat16, jnp.float32, jnp.int32
    dma = pltpu.SemaphoreType.DMA
    hbm = pl.BlockSpec(memory_space=pltpu.MemorySpace.HBM)
    n_images = tiles.shape[1]
    samples = images.shape[0]
    out = pl.pallas_call(
        functools.partial(kernel, (n_replica, n_section, n_tensor, kv_heads)),
        out_shape=jax.ShapeDtypeStruct((rows, width), bf16),
        in_specs=[hbm] * 10,
        out_specs=pl.BlockSpec(memory_space=pltpu.VMEM),
        scratch_shapes=[
            pltpu.VMEM((n_tensor, 2, half, width), bf16),
            pltpu.VMEM((2 * kv_heads, n_section, 2 * n_replica, head_dim), bf16),
            pltpu.VMEM(q_weight.shape[1:], bf16),
            pltpu.VMEM(o_weight.shape[1:], bf16),
            pltpu.VMEM((1, head_dim), f32),
            pltpu.VMEM((1, head_dim), f32),
            pltpu.SMEM((1,), f32),
            pltpu.SMEM((samples,), i32),
            pltpu.SMEM((n_images, samples), i32),
            pltpu.SMEM((n_images, samples), i32),
            pltpu.VMEM((rows, width), f32),
            pltpu.VMEM((2 * kv_heads, 2 * plane, head_dim), bf16),
            pltpu.VMEM((n_tensor, 2, 2 * plane, head_dim), bf16),
            pltpu.VMEM((n_tensor, 2 * plane, head_dim), bf16),
            pltpu.VMEM((2, rows, head_dim), bf16),
            pltpu.VMEM((2, 1, slots), i32),
            pltpu.VMEM((rows, slots), f32),
            pltpu.VMEM((rows, slots), bf16),
            pltpu.VMEM((rows, width), bf16),
            pltpu.VMEM((2, 2, rows, width), f32),
            pltpu.VMEM((turn, 2, half, width), bf16),
            pltpu.VMEM((turn - 1, 2, half, width), bf16),
            pltpu.VMEM((turn, 2, half, width), bf16),
            pltpu.VMEM((turn - 1, 2, half, width), bf16),
            dma((12,)),
            dma((2 * kv_heads,)),
            dma((n_tensor, 2)),
            dma((turn, 2)),
            dma((turn, 2)),
            dma((plane,)),
            dma((plane,)),
            dma((n_tensor,)),
            dma((kv_heads,)),
            dma((2,)),
            dma((reach + group - 1,)),
            dma((reach + group - 1,)),
            dma((turn, 2)),
            dma((turn - 1, 2)),
            dma((turn, 2)),
            dma((turn - 1, 2)),
        ],
        compiler_params=pltpu.CompilerParams(
            collective_id=0, has_side_effects=True, vmem_limit_bytes=60 * 1024 * 1024
        ),
    )(
        hidden[0], vision_kv[:, :, 0], q_weight[0], o_weight[0], q_gain, k_gain, attn_gate, images, tiles.T, text_start.T
    )
    return out[None]


def solution(mesh):
    return jax.shard_map(
        on_device,
        mesh=mesh,
        in_specs=(
            P("section", "dp", "tensor"),
            P("section", None, "tensor"),
            P("section", "tensor", None),
            P(None, None, ("dp", "section", "tensor"), None),
            P("section", None),
            P("section", None),
            P("section"),
            P(),
            P(),
            P(),
        ),
        out_specs=P("section", "dp", "tensor"),
        check_vma=False,
    )
```

```python
import functools

import jax
import jax.numpy as jnp
from jax import lax
from jax.experimental import pallas as pl
from jax.experimental.pallas import tpu as pltpu
from jax.sharding import PartitionSpec as P

TILES = 4
P_SIZE = 128
MESH = pl.DeviceIdType.MESH
PIECES = 2
EXCHANGED = 3
CHAINED = 5
BATCH = 3
LAG = 5


def kernel(
    sizes,
    hidden_hbm, kv_hbm, qw_hbm, ow_hbm, q_gain_hbm, k_gain_hbm, gate_hbm, images_hbm, tiles_hbm, start_hbm,
    out_ref,
    hid_all, kv_own, qw, ow, q_gain, k_gain, gate, images, tiles, start,
    acc, kvx, kv_all, keys, queries, limits, scores, weights, mixed, part,
    got_r, got_l, put_r, put_l, near_got_r, near_got_l, near_put_r, near_put_l,
    local_sem, kv_sem, ag_recv, ag_send_r, ag_send_l, x_recv, x_send, z_recv, z_send, own_send, chain_r, chain_l,
    rs_recv_r, rs_recv_l, rs_send_r, rs_send_l, near_recv_r, near_recv_l, near_send_r, near_send_l,
):
    n_replica, n_section, n_tensor, kv_heads = sizes
    plane = n_replica * n_section
    group = n_tensor // kv_heads
    reach = (n_tensor - group) // 2
    turn = n_tensor // 2
    last = turn - 1
    rows, width = out_ref.shape
    half = rows // 2
    piece = rows // PIECES
    head_dim = width // 2
    block = 2 * plane
    slots = n_tensor * block
    dp = lax.axis_index("dp")
    sec = lax.axis_index("section")
    t = lax.axis_index("tensor")
    me = dp * n_section + sec
    mine = t // group
    j = t % group
    base = mine * group

    def ring(offset):
        return (t + offset + n_tensor) % n_tensor

    right = ring(1)
    left = ring(-1)

    def z_dev(index):
        return (dp, sec, index)

    def plane_dev(index):
        return (index // n_section, index % n_section, t)

    barrier = pltpu.get_barrier_semaphore()

    @pl.loop(0, reach)
    def _(p):
        pl.semaphore_signal(barrier, inc=1, device_id=z_dev(ring(reach - p)), device_id_type=MESH)
        pl.semaphore_signal(barrier, inc=1, device_id=z_dev(ring(p - reach)), device_id_type=MESH)

    @pl.loop(1, plane)
    def _(p):
        pl.semaphore_signal(barrier, inc=1, device_id=plane_dev((me + p) % plane), device_id_type=MESH)

    local = [
        pltpu.make_async_copy(src, dst, local_sem.at[i])
        for i, (src, dst) in enumerate([
            *((hidden_hbm.at[pl.ds(b * piece, piece)], hid_all.at[t, b]) for b in range(PIECES)),
            (qw_hbm, qw),
            (images_hbm, images),
            (tiles_hbm, tiles),
            (start_hbm, start),
            (q_gain_hbm, q_gain),
            (k_gain_hbm, k_gain),
            (gate_hbm, gate),
            (ow_hbm, ow),
        ])
    ]
    columns = [
        pltpu.make_async_copy(
            kv_hbm.at[:, :, pl.ds(i * head_dim, head_dim)], kv_own.at[i], kv_sem.at[i]
        )
        for i in range(2 * kv_heads)
    ]
    for copy in local[:PIECES] + columns + local[PIECES:]:
        copy.start()
    acc[...] = jnp.zeros_like(acc)
    for copy in local[:PIECES] + columns + local[PIECES:]:
        copy.wait()
    pl.semaphore_wait(barrier, plane - 1 + 2 * reach)

    def ag_copy(source, b, sem, target):
        place = hid_all.at[source, b]
        return pltpu.make_async_remote_copy(
            src_ref=place, dst_ref=place, send_sem=sem, recv_sem=ag_recv.at[source, b],
            device_id=z_dev(target), device_id_type=MESH,
        )

    def ag_right(k, b):
        return ag_copy(ring(-k), b, ag_send_r.at[k % turn, b], right)

    def ag_left(k, b):
        return ag_copy(ring(k), b, ag_send_l.at[k % turn, b], left)

    def x_copy(peer, origin):
        return pltpu.make_async_remote_copy(
            src_ref=kv_own.at[:, peer % n_section, pl.ds(2 * (peer // n_section), 2)],
            dst_ref=kvx.at[:, pl.ds(2 * origin, 2)],
            send_sem=x_send.at[peer], recv_sem=x_recv.at[origin],
            device_id=plane_dev(peer), device_id_type=MESH,
        )

    own_x = pltpu.make_async_copy(
        kv_own.at[:, sec, pl.ds(2 * dp, 2)], kvx.at[:, pl.ds(2 * me, 2)], local_sem.at[-2 + local_sem.shape[0]]
    )
    own_x.start()
    for b in range(PIECES):
        ag_right(0, b).start()
        ag_left(0, b).start()

        @pl.loop(b * plane // PIECES, (b + 1) * plane // PIECES)
        def _(p):
            @pl.when(p > 0)
            def _():
                x_copy((me + p) % plane, me).start()

    column = lax.broadcasted_iota(jnp.int32, (1, slots), 1)
    position = (column % block) // 2 * n_tensor + column // block
    image_of = position // (TILES * P_SIZE)
    tile_of = position // P_SIZE % TILES
    for m in range(2):
        sample = dp * 2 + m
        limit = jnp.full((1, slots), half, jnp.int32)
        for image in range(tiles.shape[0]):
            fits = (image_of == image) & (tile_of < tiles[image, sample]) & (image < images[sample])
            limit = jnp.where(fits, start[image, sample], limit)
        limits[m] = jnp.where(column % 2 == m, limit, half)

    def z_copy(source_ref, source, sem, target):
        return pltpu.make_async_remote_copy(
            src_ref=source_ref, dst_ref=kv_all.at[source], send_sem=sem, recv_sem=z_recv.at[source],
            device_id=z_dev(target), device_id_type=MESH,
        )

    def entry(i):
        head = (mine + i) % kv_heads
        ahead = (group * head - t + n_tensor) % n_tensor
        target = group * head + (group - 1) * (ahead // (reach + 1))
        return z_copy(kvx.at[pl.ds(2 * head, 2)], t, z_send.at[i], target)

    def pass_right(i):
        src = (base - i + n_tensor) % n_tensor
        return z_copy(kv_all.at[src], src, chain_r.at[i + group - 2], right)

    def pass_left(i):
        src = (base + group - 1 + i) % n_tensor
        return z_copy(kv_all.at[src], src, chain_l.at[i + group - 2], left)

    own_block = kvx.at[pl.ds(2 * mine, 2)]
    own_right = z_copy(own_block, t, own_send.at[0], right)
    own_left = z_copy(own_block, t, own_send.at[1], left)
    own_z = pltpu.make_async_copy(own_block, kv_all.at[t], local_sem.at[-1 + local_sem.shape[0]])

    def take(source):
        raw = kv_all[source, 0].astype(jnp.float32)
        square = jnp.mean(raw * raw, axis=-1, keepdims=True)
        keys[source] = (raw * lax.rsqrt(square + 1e-05) * k_gain[...]).astype(jnp.bfloat16)

    turns = reach + LAG * (group - 1)

    def chain(n):
        i_right = n - LAG * j
        i_left = n - LAG * (group - 1 - j)
        to_right = (i_right > -j) & (i_right <= reach)
        to_left = (i_left > j - group + 1) & (i_left <= reach)

        @pl.when(to_right)
        def _():
            pass_right(i_right).wait_recv()

            @pl.when(j < group - 1)
            def _():
                pass_right(i_right).start()

            take((base - i_right + n_tensor) % n_tensor)

        @pl.when(to_left)
        def _():
            pass_left(i_left).wait_recv()

            @pl.when(j > 0)
            def _():
                pass_left(i_left).start()

            take((base + group - 1 + i_left) % n_tensor)

    def enter(q):
        entry(q).start()

        @pl.when(2 * q != kv_heads)
        def _():
            entry(kv_heads - q).start()

    def project(source):
        chunk = hid_all[source].reshape(rows, width)
        acc[...] += jnp.dot(
            chunk, qw[pl.ds(pl.multiple_of(source * width, width), width), :], preferred_element_type=jnp.float32
        )

    def ag_step(k, carry):
        def hand_on(b):
            ag_right(k, b).wait_recv()
            ag_right(k, b).start()
            ag_left(k, b).wait_recv()
            ag_left(k, b).start()

        for b in range(PIECES // 2):
            hand_on(b)
        project(ring(1 - k))

        @pl.when(k == EXCHANGED)
        def _():
            @pl.loop(1, plane)
            def _(p):
                peer = (me + p) % plane
                x_copy(peer, peer).wait_recv()

            own_x.wait()
            own_z.start()

            @pl.when(j < group - 1)
            def _():
                own_right.start()

            @pl.when(j > 0)
            def _():
                own_left.start()

        for b in range(PIECES // 2, PIECES):
            hand_on(b)

        @pl.when((k >= EXCHANGED) & (k < EXCHANGED + kv_heads // 2))
        def _():
            enter(k - EXCHANGED + 1)

        @pl.when(k > 1)
        def _():
            project(ring(k - 1))

        @pl.when(k >= CHAINED)
        def _():
            @pl.loop(0, BATCH)
            def _(n):
                chain(BATCH * (k - CHAINED) + n + 1)

        return carry

    lax.fori_loop(1, last, ag_step, 0)

    middle = PIECES // 2
    for b in range(middle):
        ag_right(last, b).wait_recv()
        ag_right(last, b).start()
        ag_left(last, middle + b).wait_recv()
        ag_left(last, middle + b).start()
    project(ring(1 - last))
    project(ring(last - 1))
    for b in range(middle):
        ag_right(last, middle + b).wait_recv()
        ag_left(last, b).wait_recv()
    project(ring(-last))
    project(ring(last))

    @pl.loop(BATCH * max(0, last - CHAINED), turns)
    def _(n):
        chain(n + 1)

    own_z.wait()
    take(t)
    for b in range(middle):
        ag_right(turn, b).wait_recv()
        ag_left(turn, middle + b).wait_recv()
    project(ring(turn))

    for h in range(2):
        raw = acc[:, h * head_dim : (h + 1) * head_dim]
        square = jnp.mean(raw * raw, axis=-1, keepdims=True)
        normal = (raw * lax.rsqrt(square + 1e-05) * q_gain[...]).astype(jnp.bfloat16)
        for m in range(2):
            queries[m, h * half : (h + 1) * half, :] = normal[m * half : (m + 1) * half]

    step_rows = 16 if half % 16 == 0 else half

    def attend(m):
        scores[...] = lax.dot_general(
            queries[m], keys[...].reshape(slots, head_dim), (((1,), (1,)), ((), ())),
            preferred_element_type=jnp.float32,
        ) * head_dim ** (-0.5)

        def soften(i, carry):
            r0 = pl.multiple_of(i * step_rows, step_rows)
            text_row = r0 % half + lax.broadcasted_iota(jnp.int32, (step_rows, slots), 0)
            seen = text_row >= limits[m]
            found = jnp.where(seen, scores[pl.ds(r0, step_rows), :], -1e30)
            top = jnp.max(found, axis=-1, keepdims=True)
            expo = jnp.where(seen, jnp.exp(found - top), 0.0)
            total = jnp.maximum(jnp.sum(expo, axis=-1, keepdims=True), 1.0)
            weights[pl.ds(r0, step_rows), :] = (expo / total).astype(jnp.bfloat16)
            return carry

        lax.fori_loop(0, rows // step_rows, soften, 0)
        both = jnp.dot(
            weights[...], kv_all[:, 1].reshape(slots, head_dim), preferred_element_type=jnp.float32
        ).astype(jnp.bfloat16)
        for h in range(2):
            mixed[m * half : (m + 1) * half, h * head_dim : (h + 1) * head_dim] = both[h * half : (h + 1) * half]

    def share(dest, span):
        return jnp.dot(
            mixed[span, :], ow[:, pl.ds(pl.multiple_of(dest * width, width), width)],
            preferred_element_type=jnp.float32,
        )

    def rs_copy(put, got, send, recv, target, k, b):
        return pltpu.make_async_remote_copy(
            src_ref=put.at[k, b], dst_ref=got.at[k, b], send_sem=send.at[k, b], recv_sem=recv.at[k, b],
            device_id=z_dev(target), device_id_type=MESH,
        )

    hops = turn // 2
    go_right = functools.partial(rs_copy, put_r, got_r, rs_send_r, rs_recv_r, ring(2))
    go_left = functools.partial(rs_copy, put_l, got_l, rs_send_l, rs_recv_l, ring(-2))
    near_right = functools.partial(rs_copy, near_put_r, near_got_r, near_send_r, near_recv_r, right)
    near_left = functools.partial(rs_copy, near_put_l, near_got_l, near_send_l, near_recv_l, left)
    spans = [slice(b * piece, (b + 1) * piece) for b in range(PIECES)]
    whole = slice(0, rows)

    def hand_right(q, b, value):
        near_put_r[q, b] = value.astype(jnp.bfloat16)
        near_right(q, b).start()

    def hand_left(q, b, value):
        near_put_l[q, b] = value.astype(jnp.bfloat16)
        near_left(q, b).start()

    def sum_right(k, b):
        near_right(hops - k, b).wait_recv()
        own = part[k % 2, 0, spans[b]] + near_got_r[hops - k, b].astype(jnp.float32)
        go_right(k - 1, b).wait_recv()
        put_r[k, b] = (got_r[k - 1, b].astype(jnp.float32) + own).astype(jnp.bfloat16)
        go_right(k, b).start()

    def sum_left(k, b):
        near_left(hops - 1 - k, b).wait_recv()
        own = part[k % 2, 1, spans[b]] + near_got_l[hops - 1 - k, b].astype(jnp.float32)
        go_left(k - 1, b).wait_recv()
        put_l[k, b] = (got_l[k - 1, b].astype(jnp.float32) + own).astype(jnp.bfloat16)
        go_left(k, b).start()

    for b in range(PIECES):
        if b * piece % half == 0:
            attend(b * piece // half)
        put_r[0, b] = share(ring(turn), spans[b]).astype(jnp.bfloat16)
        go_right(0, b).start()
        hand_left(hops - 1, b, share(ring(1 - turn), spans[b]))
        hand_right(hops - 1, b, share(ring(turn - 1), spans[b]))
    part[0, 1] = share(ring(2 - turn), whole)
    part[1, 0] = share(ring(turn - 2), whole)
    for b in range(PIECES):
        near_left(hops - 1, b).wait_recv()
        put_l[0, b] = (near_got_l[hops - 1, b].astype(jnp.float32) + part[0, 1, spans[b]]).astype(jnp.bfloat16)
        go_left(0, b).start()
    part[1, 1] = share(ring(4 - turn), whole)
    early_right = share(ring(turn - 3), whole)
    early_left = share(ring(3 - turn), whole)
    for b in range(PIECES):
        hand_right(hops - 2, b, early_right[spans[b]])
        hand_left(hops - 2, b, early_left[spans[b]])

    def rs_step(k, carry):
        for b in range(PIECES):
            sum_right(k, b)
            sum_left(k, b)
        q = hops - 2 - k
        part[(k + 1) % 2, 0] = share(ring(turn - 2 - 2 * k), whole)
        part[(k + 1) % 2, 1] = share(ring(2 * k + 4 - turn), whole)
        later_right = share(ring(2 * q + 1), whole)
        later_left = share(ring(-2 * q - 1), whole)
        for b in range(PIECES):
            hand_right(q, b, later_right[spans[b]])
            hand_left(q, b, later_left[spans[b]])
        for b in range(PIECES):
            for n in range(2):
                ag_right(2 * k - 2 + n, b).wait_send()
                ag_left(2 * k - 2 + n, b).wait_send()
            go_right(k - 1, b).wait_send()
            go_left(k - 1, b).wait_send()
            near_right(q + 1, b).wait_send()
            near_left(q + 1, b).wait_send()
        return carry

    lax.fori_loop(1, hops - 1, rs_step, 0)
    for b in range(PIECES):
        sum_right(hops - 1, b)

    for b in range(PIECES):
        for k in range(2 * (hops - 2), last):
            ag_right(k, b).wait_send()
            ag_left(k, b).wait_send()
        go_right(hops - 2, b).wait_send()
        go_left(hops - 2, b).wait_send()
        for q in (0, hops - 1):
            near_right(q, b).wait_send()
            near_left(q, b).wait_send()
    for b in range(middle):
        ag_right(last, b).wait_send()
        ag_left(last, middle + b).wait_send()

    @pl.loop(1, plane)
    def _(p):
        x_copy((me + p) % plane, me).wait_send()

    @pl.loop(1, kv_heads)
    def _(i):
        entry(i).wait_send()

    @pl.when(j < group - 1)
    def _():
        own_right.wait_send()

        @pl.loop(0, reach + j)
        def _(n):
            pass_right(reach - n).wait_send()

    @pl.when(j > 0)
    def _():
        own_left.wait_send()

        @pl.loop(0, reach + group - 1 - j)
        def _(n):
            pass_left(reach - n).wait_send()

    scale = jnp.tanh(jnp.full((1, width), gate[0], jnp.float32))
    for b in range(PIECES):
        near_left(0, b).wait_recv()
        near_right(0, b).wait_recv()
        total = part[(hops - 1) % 2, 1, spans[b]] + near_got_l[0, b].astype(jnp.float32)
        total += near_got_r[0, b].astype(jnp.float32)
        go_left(hops - 2, b).wait_recv()
        total += got_l[hops - 2, b].astype(jnp.float32)
        go_right(hops - 1, b).wait_recv()
        total += got_r[hops - 1, b].astype(jnp.float32)
        out_ref[spans[b], :] = (hid_all[t, b].astype(jnp.float32) + scale * total).astype(jnp.bfloat16)
    for b in range(PIECES):
        go_right(hops - 1, b).wait_send()


def on_device(
    hidden, q_weight, o_weight, vision_kv, q_gain, k_gain, attn_gate, images, tiles, text_start
):
    n_tensor = lax.axis_size("tensor")
    n_section = lax.axis_size("section")
    n_replica = lax.axis_size("dp")
    plane = n_section * n_replica
    head_dim = q_gain.shape[1]
    kv_heads = vision_kv.shape[3] // (2 * head_dim)
    rows, width = hidden.shape[1:]
    piece = rows // PIECES
    turn = n_tensor // 2
    hops = turn // 2
    group = n_tensor // kv_heads
    reach = (n_tensor - group) // 2
    slots = n_tensor * 2 * plane
    bf16, f32, i32 = jnp.bfloat16, jnp.float32, jnp.int32
    dma = pltpu.SemaphoreType.DMA
    hbm = pl.BlockSpec(memory_space=pltpu.MemorySpace.HBM)
    n_images = tiles.shape[1]
    samples = images.shape[0]
    out = pl.pallas_call(
        functools.partial(kernel, (n_replica, n_section, n_tensor, kv_heads)),
        out_shape=jax.ShapeDtypeStruct((rows, width), bf16),
        in_specs=[hbm] * 10,
        out_specs=pl.BlockSpec(memory_space=pltpu.VMEM),
        scratch_shapes=[
            pltpu.VMEM((n_tensor, PIECES, piece, width), bf16),
            pltpu.VMEM((2 * kv_heads, n_section, 2 * n_replica, head_dim), bf16),
            pltpu.VMEM(q_weight.shape[1:], bf16),
            pltpu.VMEM(o_weight.shape[1:], bf16),
            pltpu.VMEM((1, head_dim), f32),
            pltpu.VMEM((1, head_dim), f32),
            pltpu.SMEM((1,), f32),
            pltpu.SMEM((samples,), i32),
            pltpu.SMEM((n_images, samples), i32),
            pltpu.SMEM((n_images, samples), i32),
            pltpu.VMEM((rows, width), f32),
            pltpu.VMEM((2 * kv_heads, 2 * plane, head_dim), bf16),
            pltpu.VMEM((n_tensor, 2, 2 * plane, head_dim), bf16),
            pltpu.VMEM((n_tensor, 2 * plane, head_dim), bf16),
            pltpu.VMEM((2, rows, head_dim), bf16),
            pltpu.VMEM((2, 1, slots), i32),
            pltpu.VMEM((rows, slots), f32),
            pltpu.VMEM((rows, slots), bf16),
            pltpu.VMEM((rows, width), bf16),
            pltpu.VMEM((2, 2, rows, width), f32),
            pltpu.VMEM((hops, PIECES, piece, width), bf16),
            pltpu.VMEM((hops - 1, PIECES, piece, width), bf16),
            pltpu.VMEM((hops, PIECES, piece, width), bf16),
            pltpu.VMEM((hops - 1, PIECES, piece, width), bf16),
            pltpu.VMEM((hops, PIECES, piece, width), bf16),
            pltpu.VMEM((hops, PIECES, piece, width), bf16),
            pltpu.VMEM((hops, PIECES, piece, width), bf16),
            pltpu.VMEM((hops, PIECES, piece, width), bf16),
            dma((PIECES + 10,)),
            dma((2 * kv_heads,)),
            dma((n_tensor, PIECES)),
            dma((turn, PIECES)),
            dma((turn, PIECES)),
            dma((plane,)),
            dma((plane,)),
            dma((n_tensor,)),
            dma((kv_heads,)),
            dma((2,)),
            dma((reach + group - 1,)),
            dma((reach + group - 1,)),
            dma((hops, PIECES)),
            dma((hops - 1, PIECES)),
            dma((hops, PIECES)),
            dma((hops - 1, PIECES)),
            dma((hops, PIECES)),
            dma((hops, PIECES)),
            dma((hops, PIECES)),
            dma((hops, PIECES)),
        ],
        compiler_params=pltpu.CompilerParams(
            collective_id=0, has_side_effects=True, vmem_limit_bytes=60 * 1024 * 1024
        ),
    )(
        hidden[0], vision_kv[:, :, 0], q_weight[0], o_weight[0], q_gain, k_gain, attn_gate, images, tiles.T, text_start.T
    )
    return out[None]


def solution(mesh):
    return jax.shard_map(
        on_device,
        mesh=mesh,
        in_specs=(
            P("section", "dp", "tensor"),
            P("section", None, "tensor"),
            P("section", "tensor", None),
            P(None, None, ("dp", "section", "tensor"), None),
            P("section", None),
            P("section", None),
            P("section"),
            P(),
            P(),
            P(),
        ),
        out_specs=P("section", "dp", "tensor"),
        check_vma=False,
    )
```
